32 devices in a mesh: dp: 8 (over z, core), width: 4 (over y, x).
Axes of the slice: x: 2, y: 2, z: 4, core: 2. Of those that a mesh axis runs over, the one named last changes fastest.
Arguments:
- inputs: bfloat16 [1536, 4, 512], P('dp', 'width'), may hold values from -6 to 6
- block_weights: bfloat16 [4, 512, 3, 512], P('width'), may hold values from -0.15625 to 0.15625
- low_left: bfloat16 [4, 512, 256], P('width'), may hold values from -0.125 to 0.125
- low_right: bfloat16 [4, 256, 512], P('width'), may hold values from -0.375 to 0.375
- out_grad: bfloat16 [1536, 4, 512], P('dp', 'width'), may hold values from -6 to 6
Outputs:
- activations: bfloat16 [1536, 4, 512], P('dp', 'width')
- in_grad: bfloat16 [1536, 4, 512], P('dp', 'width')
- block_grad: float32 [4, 512, 3, 512], P('width', 'dp')
- left_grad: float32 [4, 512, 256], P('width', 'dp')
- right_grad: float32 [4, 256, 512], P('width', 'dp')
The draws below stay inside these ranges and needn't reach their ends.
All inputs are finite; a program needn't handle non-finite values.
Results may differ from the reference program's by a relative error of at most 0.0061.
Values may be sent and summed in bfloat16 or wider, within the bound.
A program may use at most 64 MiB of HBM per device.

```python
import jax
import jax.numpy as jnp
from jax import lax

BLOCK = 512
OUT_WIN = 512
RANK = 256
BLOCKS = 4
LEVELS = 2
D = 2048
TOKENS = 1536
N_WIDTH = 4


def block_levels(own_key, dims, shards, least, top_value):
    def one(position, shards_of):
        heights = jax.random.uniform(jax.random.fold_in(jax.random.fold_in(own_key, 6), position), (shards_of,), jnp.float32, least / len(shards), top_value / len(shards))
        return jnp.repeat(jnp.exp(heights), dims[position] // shards_of).reshape((-1,) + (1,) * (len(dims) - position - 1))

    level = one(*shards[0])
    for cut in shards[1:]:
        level = level * one(*cut)
    return level


def noise(key, shape, spread, limit, shards=(), held_as=jnp.bfloat16):
    result = jax.random.normal(key, shape, jnp.float32) * spread
    if len(shards) > 0:
        result = block_levels(key, shape, shards, -0.22, 0.18) * result
    return jnp.clip(result, min=-limit, max=limit).astype(held_as)


def setup_inputs(seed: int = 0) -> dict:
    arg_keys = jax.random.split(jax.random.key(seed), 6)
    inputs = noise(arg_keys[0], (TOKENS, BLOCKS, BLOCK), 1.0, 6.0, ((0, 8), (1, 4)))
    block_weights = noise(arg_keys[1], (BLOCKS, OUT_WIN, LEVELS + 1, BLOCK), ((LEVELS + 1) * BLOCK) ** -0.5, 0.15625, ((0, 4),))
    low_left = noise(arg_keys[2], (BLOCKS, BLOCK, RANK), D ** -0.5, 0.125, ((0, 4),))
    low_right = noise(arg_keys[3], (BLOCKS, RANK, OUT_WIN), RANK ** -0.5, 0.375, ((0, 4),))
    out_grad = noise(arg_keys[4], (TOKENS, BLOCKS, OUT_WIN), 1.0, 6.0, ((0, 8), (1, 4)))
    return {"inputs": inputs, "block_weights": block_weights, "low_left": low_left, "low_right": low_right, "out_grad": out_grad}


root_half = 0.7071067811865476
inv_root_two_pi = 0.3989422804014327


def gelu_value(pre):
    return 0.5 * pre * (1.0 + lax.erf(pre * root_half))


def gelu_slope(pre):
    return 0.5 * (1.0 + lax.erf(pre * root_half)) + pre * jnp.exp(-0.5 * pre * pre) * inv_root_two_pi


def reference(inputs, block_weights, low_left, low_right, out_grad):
    blocks = N_WIDTH
    distances = [0] + [1 << level for level in range(LEVELS)]
    scale = 1.0 / (float(TOKENS) ** 0.5)
    latent_sum = jnp.zeros((inputs.shape[0], RANK), jnp.float32)
    for block in range(blocks):
        latent_sum = latent_sum + jnp.dot(inputs[:, block], low_left[block], preferred_element_type=jnp.float32)
    latent = latent_sum.astype(jnp.bfloat16)
    acts_list = []
    hidden_list = []
    right_list = []
    back_list = []
    block_list = []
    latent_grad_sum = jnp.zeros((inputs.shape[0], RANK), jnp.float32)
    for block in range(blocks):
        pre = jnp.dot(latent, low_right[block], preferred_element_type=jnp.float32)
        for level in range(LEVELS + 1):
            mate_x = inputs[:, block ^ distances[level]]
            pre = pre + jnp.dot(mate_x, block_weights[block, :, level, :].T, preferred_element_type=jnp.float32)
        acts_list.append(gelu_value(pre).astype(jnp.bfloat16))
        hidden = (out_grad[:, block].astype(jnp.float32) * gelu_slope(pre)).astype(jnp.bfloat16)
        hidden_list.append(hidden)
        latent_grad_sum = latent_grad_sum + jnp.dot(hidden, low_right[block].T, preferred_element_type=jnp.float32)
        backs = []
        for level in range(LEVELS + 1):
            backs.append(jnp.dot(hidden, block_weights[block, :, level, :], preferred_element_type=jnp.float32).astype(jnp.bfloat16))
        back_list.append(backs)
        right_list.append(jnp.dot(latent.T, hidden, preferred_element_type=jnp.float32) * scale)
        terms = []
        for level in range(LEVELS + 1):
            mate_x = inputs[:, block ^ distances[level]]
            terms.append(jnp.dot(hidden.T, mate_x, preferred_element_type=jnp.float32) * scale)
        block_list.append(jnp.stack(terms, axis=1))
    latent_grad = latent_grad_sum.astype(jnp.bfloat16)
    in_list = []
    left_list = []
    for block in range(blocks):
        own_x = inputs[:, block]
        total = jnp.dot(hidden_list[block], block_weights[block, :, 0, :], preferred_element_type=jnp.float32)
        total = total + jnp.dot(latent_grad, low_left[block].T, preferred_element_type=jnp.float32)
        for level in range(1, LEVELS + 1):
            total = total + back_list[block ^ distances[level]][level].astype(jnp.float32)
        in_list.append(total.astype(jnp.bfloat16))
        left_list.append(jnp.dot(own_x.T, latent_grad, preferred_element_type=jnp.float32) * scale)
    activations = jnp.stack(acts_list, axis=1)
    in_grad = jnp.stack(in_list, axis=1)
    block_grad = jnp.stack(block_list, axis=0)
    left_grad = jnp.stack(left_list, axis=0)
    right_grad = jnp.stack(right_list, axis=0)
    return activations, in_grad, block_grad, left_grad, right_grad
```

```python
import functools
import math

import jax
import jax.numpy as jnp
from jax import lax
from jax.experimental import pallas as pl
from jax.experimental.pallas import tpu as pltpu
from jax.sharding import PartitionSpec as P

root_half = 0.7071067811865476
inv_root_two_pi = 0.3989422804014327


def swapped(array, axis, apart):
    return lax.ppermute(array, axis, [(i, i ^ 1 << apart) for i in range(lax.axis_size(axis))])


def gelu_value(pre):
    return 0.5 * pre * (1.0 + lax.erf(pre * root_half))


def gelu_slope(pre):
    return (
        0.5 * (1.0 + lax.erf(pre * root_half)) + pre * jnp.exp(-0.5 * pre * pre) * inv_root_two_pi
    )


def plain_shards(inputs, block_weights, low_left, low_right, out_grad):
    own_x = inputs[:, 0]
    weights = block_weights[0]
    left = low_left[0]
    right = low_right[0]
    grad_out = out_grad[:, 0]
    levels = lax.axis_size("width").bit_length() - 1
    block_size = own_x.shape[1]
    scale = 1.0 / math.sqrt(own_x.shape[0] * lax.axis_size("dp"))
    pieces = [own_x]
    for bit in range(levels):
        pieces.append(swapped(own_x, "width", bit))
    all_x = jnp.stack(pieces, axis=1)
    latent = lax.psum(jnp.dot(own_x, left, preferred_element_type=jnp.float32), "width").astype(
        jnp.bfloat16
    )
    pre = lax.dot_general(
        all_x, weights, (((1, 2), (1, 2)), ((), ())), preferred_element_type=jnp.float32
    )
    pre = pre + jnp.dot(latent, right, preferred_element_type=jnp.float32)
    activations = gelu_value(pre).astype(jnp.bfloat16)
    hidden = (grad_out.astype(jnp.float32) * gelu_slope(pre)).astype(jnp.bfloat16)
    latent_term = lax.dot_general(
        hidden, right, (((1,), (1,)), ((), ())), preferred_element_type=jnp.float32
    )
    latent_grad = lax.psum(latent_term, "width").astype(jnp.bfloat16)
    partner_w = weights[:, 1:, :].reshape(weights.shape[0], levels * block_size)
    backs = jnp.dot(hidden, partner_w, preferred_element_type=jnp.float32).astype(jnp.bfloat16)
    returned = jnp.zeros(own_x.shape, jnp.float32)
    for bit in range(levels):
        piece = backs[:, bit * block_size : (bit + 1) * block_size]
        returned = returned + swapped(piece, "width", bit).astype(jnp.float32)
    own_back = jnp.dot(hidden, weights[:, 0, :], preferred_element_type=jnp.float32)
    own_back = own_back + lax.dot_general(
        latent_grad, left, (((1,), (1,)), ((), ())), preferred_element_type=jnp.float32
    )
    in_grad = (own_back + returned).astype(jnp.bfloat16)
    left_term = (
        lax.dot_general(
            own_x, latent_grad, (((0,), (0,)), ((), ())), preferred_element_type=jnp.float32
        )
        * scale
    )
    right_term = (
        lax.dot_general(
            latent, hidden, (((0,), (0,)), ((), ())), preferred_element_type=jnp.float32
        )
        * scale
    )
    block_term = (
        lax.dot_general(hidden, all_x, (((0,), (0,)), ((), ())), preferred_element_type=jnp.float32)
        * scale
    )
    block_grad, left_grad, right_grad = (
        lax.psum_scatter(block_term, "dp", scatter_dimension=0, tiled=True),
        lax.psum_scatter(left_term, "dp", scatter_dimension=0, tiled=True),
        lax.psum_scatter(right_term, "dp", scatter_dimension=0, tiled=True),
    )
    return (
        activations[:, None],
        in_grad[:, None],
        block_grad[None],
        left_grad[None],
        right_grad[None],
    )


f32 = jnp.float32
bf16 = jnp.bfloat16


def dot_nn(a, b):
    return jnp.dot(a, b, preferred_element_type=f32)


def dot_nt(a, b):
    return lax.dot_general(a, b, (((1,), (1,)), ((), ())), preferred_element_type=f32)


def remote(src, dst, send, recv, dp, width):
    return pltpu.make_async_remote_copy(
        src_ref=src,
        dst_ref=dst,
        send_sem=send,
        recv_sem=recv,
        device_id={"dp": dp, "width": width},
        device_id_type=pl.DeviceIdType.MESH,
    )


def step_kernel(
    n_dp, n_width, scale,
    x_hbm, w_hbm, left_hbm, right_hbm, g_hbm,
    act_out, in_out, block_out, left_out, right_out,
    x, w, left, right, g,
    xs, lat_own, lat_got, lg_own, lg_got, hidden, x_t, h_t, lat_t,
    back_own, back_got, pre, own_back,
    main_away, main_own, main_core, main_send, main_lo, main_hi, main_sum,
    low_away, low_own, low_core, low_send, low_lo, low_hi, low_sum,
    load_sem, x_send, x_recv, lat_send, lat_recv, lg_send, lg_recv, back_send, back_recv,
    core_send, core_recv, line_send, lo_recv, hi_recv,
):
    levels = n_width.bit_length() - 1
    chips = n_dp // 2
    dp = lax.axis_index("dp")
    me = lax.axis_index("width")
    chip, core = dp // 2, dp % 2
    other_core = 1 - core
    twin = dp + 1 - 2 * core

    def mate(k):
        at = me
        for bit in range(levels):
            if k >> bit & 1:
                at = at + (1 << bit) * (1 - 2 * ((me // (1 << bit)) % 2))
        return at

    barrier = pltpu.get_barrier_semaphore()

    def greet(to_dp, to_width):
        pl.semaphore_signal(
            barrier,
            inc=1,
            device_id={"dp": to_dp, "width": to_width},
            device_id_type=pl.DeviceIdType.MESH,
        )

    for k in range(1, n_width):
        greet(dp, mate(k))
    greet(twin, me)

    @pl.when(chip > 0)
    def _():
        greet(dp - 2, me)

    @pl.when(chip < chips - 1)
    def _():
        greet(dp + 2, me)

    loads = [
        pltpu.make_async_copy(src, dst, load_sem.at[i])
        for i, (src, dst) in enumerate(
            ((x_hbm, x), (left_hbm, left), (w_hbm, w), (right_hbm, right), (g_hbm, g))
        )
    ]
    for load in loads:
        load.start()

    ends = jnp.where(chip == 0, 1, 0) + jnp.where(chip == chips - 1, 1, 0)
    pl.semaphore_wait(barrier, n_width + 2 - ends)

    loads[0].wait()
    x_copies = [
        remote(x, xs.at[bit], x_send.at[bit], x_recv.at[bit], dp, mate(1 << bit))
        for bit in range(levels)
    ]
    loads[1].wait()
    lat_mine = dot_nn(x[...], left[...])
    lat_own[...] = lat_mine.astype(bf16)
    lat_copies = [
        remote(lat_own, lat_got.at[k - 1], lat_send.at[k - 1], lat_recv.at[k - 1], dp, mate(k))
        for k in range(1, n_width)
    ]
    for copy in lat_copies:
        copy.start()
    for copy in x_copies:
        copy.start()
    loads[2].wait()
    pre[...] = dot_nt(x[...], w[0])
    x_t[...] = x[...].astype(f32).T.astype(bf16).reshape(x_t.shape)
    loads[3].wait()
    loads[4].wait()
    for copy in lat_copies:
        copy.wait_recv()
    lat_sum = lat_mine
    for k in range(n_width - 1):
        lat_sum = lat_sum + lat_got[k].astype(f32)
    latent = lat_sum.astype(bf16)
    lat_t[...] = lat_sum.T.astype(bf16).reshape(lat_t.shape)
    pre[...] += dot_nn(latent, right[...])
    for bit in range(levels):
        x_copies[bit].wait_recv()
        pre[...] += dot_nt(xs[bit], w[bit + 1])

    v = pre[...]
    half = 0.5 * (1.0 + lax.erf(v * root_half))
    act_out[...] = (v * half).astype(bf16)
    slope = half + v * jnp.exp(-0.5 * v * v) * inv_root_two_pi
    hid = g[...].astype(f32) * slope
    hidden[...] = hid.astype(bf16)
    h = hidden[...]
    lg_mine = dot_nt(h, right[...])
    lg_own[...] = lg_mine.astype(bf16)
    lg_copies = [
        remote(lg_own, lg_got.at[k - 1], lg_send.at[k - 1], lg_recv.at[k - 1], dp, mate(k))
        for k in range(1, n_width)
    ]
    for copy in lg_copies:
        copy.start()
    h_t[...] = h.astype(f32).T.astype(bf16).reshape(h_t.shape)

    ob, rb = h_t.shape[2], lat_t.shape[2]
    rows = h_t.shape[3]

    def main_terms(which, out_ref):
        lhs = h_t[:, which].reshape(chips * ob, rows)
        for level in range(levels + 1):
            rhs = x[...] if level == 0 else xs[level - 1]
            term = dot_nn(lhs, rhs).astype(out_ref.dtype)
            out_ref[:, level * ob : (level + 1) * ob, :] = term.reshape(chips, ob, term.shape[1])
        lhs = lat_t[:, which].reshape(chips * rb, rows)
        term = dot_nn(lhs, hidden[...]).astype(out_ref.dtype)
        out_ref[:, (levels + 1) * ob :, :] = term.reshape(chips, rb, term.shape[1])

    far_first = []
    for k in range((chips + 1) // 2):
        far_first += [chips - 1 - k, k] if chips - 1 - k != k else [k]
    away = (main_away, low_away)
    own = (main_own, low_own)
    got_core = (main_core, low_core)
    sends = (main_send, low_send)
    got_lo = (main_lo, low_lo)
    got_hi = (main_hi, low_hi)
    sums = (main_sum, low_sum)

    def core_copy(s, c):
        return remote(
            away[s].at[c], got_core[s].at[c], core_send.at[s, c], core_recv.at[s, c], twin, me
        )

    def up_copy(s, c, to):
        return remote(
            sends[s].at[c], got_lo[s].at[c], line_send.at[s, c], lo_recv.at[s, c], to, me
        )

    def down_copy(s, c, to):
        return remote(
            sends[s].at[c], got_hi[s].at[c], line_send.at[s, c], hi_recv.at[s, c], to, me
        )

    def pair_sum(s, c):
        core_copy(s, c).wait_recv()
        return own[s][c] + got_core[s][c].astype(f32)

    def first_hops(s):
        for k in range(chips - 1):
            c = chips - 1 - k

            @pl.when(chip == 0)
            def _():
                sends[s][c] = pair_sum(s, c).astype(bf16)
                up_copy(s, c, dp + 2).start()

            @pl.when(chip == chips - 1)
            def _():
                sends[s][k] = pair_sum(s, k).astype(bf16)
                down_copy(s, k, dp - 2).start()

    def later_hops(s, k):
        c = chips - 1 - k

        @pl.when((chip > 0) & (chip < c))
        def _():
            total = pair_sum(s, c)
            up_copy(s, c, dp + 2).wait_recv()
            sends[s][c] = (total + got_lo[s][c].astype(f32)).astype(bf16)
            up_copy(s, c, dp + 2).start()

        @pl.when((chip < chips - 1) & (chip > k))
        def _():
            total = pair_sum(s, k)
            down_copy(s, k, dp - 2).wait_recv()
            sends[s][k] = (total + got_hi[s][k].astype(f32)).astype(bf16)
            down_copy(s, k, dp - 2).start()

    def finish(s):
        sums[s][...] = pair_sum(s, chip)

        @pl.when(chip > 0)
        def _():
            up_copy(s, chip, dp - 2).wait_recv()
            sums[s][...] += got_lo[s][chip].astype(f32)

        @pl.when(chip < chips - 1)
        def _():
            down_copy(s, chip, dp + 2).wait_recv()
            sums[s][...] += got_hi[s][chip].astype(f32)

    main_terms(other_core, main_away)
    for c in far_first:
        core_copy(0, c).start()
    main_terms(core, main_own)
    first_hops(0)

    back_copies = []
    for bit in range(levels):
        back_own[bit] = dot_nn(hidden[...], w[bit + 1]).astype(bf16)
        copy = remote(
            back_own.at[bit], back_got.at[bit], back_send.at[bit], back_recv.at[bit],
            dp, mate(1 << bit),
        )
        copy.start()
        back_copies.append(copy)

    for copy in lg_copies:
        copy.wait_recv()
    for k in range(n_width - 1):
        lg_mine = lg_mine + lg_got[k].astype(f32)
    latent_grad = lg_mine.astype(bf16)

    def low_terms(which, out_ref):
        lhs = x_t[:, which].reshape(chips * x_t.shape[2], rows)
        term = dot_nn(lhs, latent_grad).astype(out_ref.dtype)
        out_ref[...] = term.reshape(out_ref.shape)

    low_terms(other_core, low_away)
    for c in far_first:
        core_copy(1, c).start()
    low_terms(core, low_own)
    first_hops(1)
    own_back[...] = dot_nn(hidden[...], w[0]) + dot_nt(latent_grad, left[...])
    for k in range(chips - 2):
        later_hops(0, k)
    for k in range(chips - 2):
        later_hops(1, k)
    total = own_back[...]
    for bit in range(levels):
        back_copies[bit].wait_recv()
        total = total + back_got[bit].astype(f32)
    in_out[...] = total.astype(bf16)
    finish(0)
    for level in range(levels + 1):
        block_out[level] = main_sum[level * ob : (level + 1) * ob, :] * scale
    right_out[...] = main_sum[(levels + 1) * ob :, :] * scale
    finish(1)
    left_out[...] = low_sum[...] * scale

    for copy in x_copies + lat_copies + lg_copies + back_copies:
        copy.wait_send()
    for s in range(2):
        for c in range(chips):
            core_copy(s, c).wait_send()

            @pl.when(chip != c)
            def _():
                up_copy(s, c, twin).wait_send()


def shards(inputs, block_weights, low_left, low_right, out_grad):
    n_dp, n_width = lax.axis_size("dp"), lax.axis_size("width")
    levels = n_width.bit_length() - 1
    rows, _, width_in = inputs.shape
    width_out = block_weights.shape[1]
    rank = low_left.shape[2]
    ob, ib, rb = width_out // n_dp, width_in // n_dp, rank // n_dp
    fits = n_dp % 2 == 0 and rows % 16 == 0 and width_in == width_out
    if not fits or ob % 16 or ib % 16 or rb % 16 or width_in % 128 or rank % 128:
        return plain_shards(inputs, block_weights, low_left, low_right, out_grad)
    chips = n_dp // 2
    scale = 1.0 / math.sqrt(rows * n_dp)
    main = (levels + 1) * ob + rb
    vm, dma = pltpu.VMEM, pltpu.SemaphoreType.DMA

    def line_scratch(r, c):
        return [
            vm((chips, r, c), bf16),
            vm((chips, r, c), f32),
            vm((chips, r, c), bf16),
            vm((chips, r, c), bf16),
            vm((chips, r, c), bf16),
            vm((chips, r, c), bf16),
            vm((r, c), f32),
        ]

    outs = pl.pallas_call(
        functools.partial(step_kernel, n_dp, n_width, scale),
        out_shape=(
            jax.ShapeDtypeStruct((rows, width_out), bf16),
            jax.ShapeDtypeStruct((rows, width_in), bf16),
            jax.ShapeDtypeStruct((levels + 1, ob, width_in), f32),
            jax.ShapeDtypeStruct((ib, rank), f32),
            jax.ShapeDtypeStruct((rb, width_out), f32),
        ),
        in_specs=[pl.BlockSpec(memory_space=pltpu.HBM)] * 5,
        out_specs=(pl.BlockSpec(memory_space=pltpu.VMEM),) * 5,
        scratch_shapes=[
            vm((rows, width_in), bf16),
            vm((levels + 1, width_out, width_in), bf16),
            vm((width_in, rank), bf16),
            vm((rank, width_out), bf16),
            vm((rows, width_out), bf16),
            vm((levels, rows, width_in), bf16),
            vm((rows, rank), bf16),
            vm((n_width - 1, rows, rank), bf16),
            vm((rows, rank), bf16),
            vm((n_width - 1, rows, rank), bf16),
            vm((rows, width_out), bf16),
            vm((chips, 2, ib, rows), bf16),
            vm((chips, 2, ob, rows), bf16),
            vm((chips, 2, rb, rows), bf16),
            vm((levels, rows, width_in), bf16),
            vm((levels, rows, width_in), bf16),
            vm((rows, width_out), f32),
            vm((rows, width_in), f32),
            *line_scratch(main, width_in),
            *line_scratch(ib, rank),
            dma((5,)),
            dma((levels,)),
            dma((levels,)),
            dma((n_width - 1,)),
            dma((n_width - 1,)),
            dma((n_width - 1,)),
            dma((n_width - 1,)),
            dma((levels,)),
            dma((levels,)),
            dma((2, chips)),
            dma((2, chips)),
            dma((2, chips)),
            dma((2, chips)),
            dma((2, chips)),
        ],
        compiler_params=pltpu.CompilerParams(
            collective_id=0, has_side_effects=True, vmem_limit_bytes=40 * 1024 * 1024
        ),
    )(
        inputs[:, 0],
        block_weights[0].transpose(1, 0, 2),
        low_left[0],
        low_right[0],
        out_grad[:, 0],
    )
    act, in_grad, block, left, right = outs
    return (
        act[:, None],
        in_grad[:, None],
        block.transpose(1, 0, 2)[None],
        left[None],
        right[None],
    )


def solution(mesh):
    placed = (
        P("dp", "width", None),
        P("width", None, None, None),
        P("width", None, None),
        P("width", None, None),
        P("dp", "width", None),
    )
    return jax.shard_map(
        shards,
        mesh=mesh,
        in_specs=placed,
        out_specs=(
            P("dp", "width", None),
            P("dp", "width", None),
            P("width", "dp", None, None),
            P("width", "dp", None),
            P("width", "dp", None),
        ),
        check_vma=False,
    )
```

```python
import functools
import math

import jax
import jax.numpy as jnp
from jax import lax
from jax.experimental import pallas as pl
from jax.experimental.pallas import tpu as pltpu
from jax.sharding import PartitionSpec as P

root_half = 0.7071067811865476
inv_root_two_pi = 0.3989422804014327


def swapped(array, axis, apart):
    return lax.ppermute(array, axis, [(i, i ^ 1 << apart) for i in range(lax.axis_size(axis))])


def gelu_value(pre):
    return 0.5 * pre * (1.0 + lax.erf(pre * root_half))


def gelu_slope(pre):
    return (
        0.5 * (1.0 + lax.erf(pre * root_half)) + pre * jnp.exp(-0.5 * pre * pre) * inv_root_two_pi
    )


def plain_shards(inputs, block_weights, low_left, low_right, out_grad):
    own_x = inputs[:, 0]
    weights = block_weights[0]
    left = low_left[0]
    right = low_right[0]
    grad_out = out_grad[:, 0]
    levels = lax.axis_size("width").bit_length() - 1
    block_size = own_x.shape[1]
    scale = 1.0 / math.sqrt(own_x.shape[0] * lax.axis_size("dp"))
    pieces = [own_x]
    for bit in range(levels):
        pieces.append(swapped(own_x, "width", bit))
    all_x = jnp.stack(pieces, axis=1)
    latent = lax.psum(jnp.dot(own_x, left, preferred_element_type=jnp.float32), "width").astype(
        jnp.bfloat16
    )
    pre = lax.dot_general(
        all_x, weights, (((1, 2), (1, 2)), ((), ())), preferred_element_type=jnp.float32
    )
    pre = pre + jnp.dot(latent, right, preferred_element_type=jnp.float32)
    activations = gelu_value(pre).astype(jnp.bfloat16)
    hidden = (grad_out.astype(jnp.float32) * gelu_slope(pre)).astype(jnp.bfloat16)
    latent_term = lax.dot_general(
        hidden, right, (((1,), (1,)), ((), ())), preferred_element_type=jnp.float32
    )
    latent_grad = lax.psum(latent_term, "width").astype(jnp.bfloat16)
    partner_w = weights[:, 1:, :].reshape(weights.shape[0], levels * block_size)
    backs = jnp.dot(hidden, partner_w, preferred_element_type=jnp.float32).astype(jnp.bfloat16)
    returned = jnp.zeros(own_x.shape, jnp.float32)
    for bit in range(levels):
        piece = backs[:, bit * block_size : (bit + 1) * block_size]
        returned = returned + swapped(piece, "width", bit).astype(jnp.float32)
    own_back = jnp.dot(hidden, weights[:, 0, :], preferred_element_type=jnp.float32)
    own_back = own_back + lax.dot_general(
        latent_grad, left, (((1,), (1,)), ((), ())), preferred_element_type=jnp.float32
    )
    in_grad = (own_back + returned).astype(jnp.bfloat16)
    left_term = (
        lax.dot_general(
            own_x, latent_grad, (((0,), (0,)), ((), ())), preferred_element_type=jnp.float32
        )
        * scale
    )
    right_term = (
        lax.dot_general(
            latent, hidden, (((0,), (0,)), ((), ())), preferred_element_type=jnp.float32
        )
        * scale
    )
    block_term = (
        lax.dot_general(hidden, all_x, (((0,), (0,)), ((), ())), preferred_element_type=jnp.float32)
        * scale
    )
    block_grad, left_grad, right_grad = (
        lax.psum_scatter(block_term, "dp", scatter_dimension=0, tiled=True),
        lax.psum_scatter(left_term, "dp", scatter_dimension=0, tiled=True),
        lax.psum_scatter(right_term, "dp", scatter_dimension=0, tiled=True),
    )
    return (
        activations[:, None],
        in_grad[:, None],
        block_grad[None],
        left_grad[None],
        right_grad[None],
    )


f32 = jnp.float32
bf16 = jnp.bfloat16


def dot_nn(a, b):
    return jnp.dot(a, b, preferred_element_type=f32)


def dot_nt(a, b):
    return lax.dot_general(a, b, (((1,), (1,)), ((), ())), preferred_element_type=f32)


def remote(src, dst, send, recv, dp, width):
    return pltpu.make_async_remote_copy(
        src_ref=src,
        dst_ref=dst,
        send_sem=send,
        recv_sem=recv,
        device_id={"dp": dp, "width": width},
        device_id_type=pl.DeviceIdType.MESH,
    )


def step_kernel(
    n_dp, n_width, scale,
    x_hbm, w_hbm, left_hbm, right_hbm, g_hbm,
    act_out, in_out, block_out, left_out, right_out,
    x, w, left, right, g,
    xs, lat_own, lat_got, lg_own, lg_got, hidden, x_t, h_t, lat_t,
    back_own, back_got, pre, own_back,
    main_away, main_own, main_core, main_send, main_lo, main_hi,
    low_away, low_own, low_core, low_send, low_lo, low_hi,
    load_sem, x_send, x_recv, lat_send, lat_recv, lg_send, lg_recv, back_send, back_recv,
    core_send, core_recv, line_send, lo_recv, hi_recv,
):
    levels = n_width.bit_length() - 1
    chips = n_dp // 2
    dp = lax.axis_index("dp")
    me = lax.axis_index("width")
    chip, core = dp // 2, dp % 2
    other_core = 1 - core
    twin = dp + 1 - 2 * core

    def mate(k):
        at = me
        for bit in range(levels):
            if k >> bit & 1:
                at = at + (1 << bit) * (1 - 2 * ((me // (1 << bit)) % 2))
        return at

    barrier = pltpu.get_barrier_semaphore()

    def greet(to_dp, to_width):
        pl.semaphore_signal(
            barrier,
            inc=1,
            device_id={"dp": to_dp, "width": to_width},
            device_id_type=pl.DeviceIdType.MESH,
        )

    for k in range(1, n_width):
        greet(dp, mate(k))
    greet(twin, me)

    @pl.when(chip > 0)
    def _():
        greet(dp - 2, me)

    @pl.when(chip < chips - 1)
    def _():
        greet(dp + 2, me)

    loads = [
        pltpu.make_async_copy(src, dst, load_sem.at[i])
        for i, (src, dst) in enumerate(
            ((x_hbm, x), (left_hbm, left), (w_hbm, w), (right_hbm, right), (g_hbm, g))
        )
    ]
    for load in loads:
        load.start()

    ends = jnp.where(chip == 0, 1, 0) + jnp.where(chip == chips - 1, 1, 0)
    pl.semaphore_wait(barrier, n_width + 2 - ends)

    loads[0].wait()
    x_copies = [
        remote(x, xs.at[bit], x_send.at[bit], x_recv.at[bit], dp, mate(1 << bit))
        for bit in range(levels)
    ]
    loads[1].wait()
    lat_mine = dot_nn(x[...], left[...])
    lat_own[...] = lat_mine.astype(bf16)
    lat_copies = [
        remote(lat_own, lat_got.at[k - 1], lat_send.at[k - 1], lat_recv.at[k - 1], dp, mate(k))
        for k in range(1, n_width)
    ]
    for copy in lat_copies:
        copy.start()
    for copy in x_copies:
        copy.start()
    loads[2].wait()
    pre[...] = dot_nt(x[...], w[0])
    x_t[...] = x[...].astype(f32).T.astype(bf16).reshape(x_t.shape)
    loads[3].wait()
    loads[4].wait()
    for copy in lat_copies:
        copy.wait_recv()
    lat_sum = lat_mine
    for k in range(n_width - 1):
        lat_sum = lat_sum + lat_got[k].astype(f32)
    latent = lat_sum.astype(bf16)
    lat_t[...] = lat_sum.T.astype(bf16).reshape(lat_t.shape)
    pre[...] += dot_nn(latent, right[...])
    for bit in range(levels):
        x_copies[bit].wait_recv()
        pre[...] += dot_nt(xs[bit], w[bit + 1])

    v = pre[...]
    half = 0.5 * (1.0 + lax.erf(v * root_half))
    act_out[...] = (v * half).astype(bf16)
    slope = half + v * jnp.exp(-0.5 * v * v) * inv_root_two_pi
    hid = g[...].astype(f32) * slope
    hidden[...] = hid.astype(bf16)
    h = hidden[...]
    lg_mine = dot_nt(h, right[...])
    lg_own[...] = lg_mine.astype(bf16)
    lg_copies = [
        remote(lg_own, lg_got.at[k - 1], lg_send.at[k - 1], lg_recv.at[k - 1], dp, mate(k))
        for k in range(1, n_width)
    ]
    for copy in lg_copies:
        copy.start()
    h_t[...] = h.astype(f32).T.astype(bf16).reshape(h_t.shape)

    ob, rb = h_t.shape[2], lat_t.shape[2]
    rows = h_t.shape[3]

    last = levels + 1

    def main_terms(which, out_ref, level):
        lhs = h_t[:, which].reshape(chips * ob, rows)
        rhs = x[...] if level == 0 else xs[level - 1]
        term = dot_nn(lhs, rhs).astype(out_ref.dtype)
        out_ref[:, level * ob : (level + 1) * ob, :] = term.reshape(chips, ob, term.shape[1])
        if level == levels:
            lhs = lat_t[:, which].reshape(chips * rb, rows)
            term = dot_nn(lhs, hidden[...]).astype(out_ref.dtype)
            out_ref[:, last * ob :, :] = term.reshape(chips, rb, term.shape[1])

    far_first = []
    for k in range((chips + 1) // 2):
        far_first += [chips - 1 - k, k] if chips - 1 - k != k else [k]

    def part(main_ref, low_ref, s, c):
        if s == last:
            return low_ref.at[c]
        top = (s + 1) * ob + (rb if s == levels else 0)
        return main_ref.at[c, s * ob : top]

    def core_copy(s, c):
        return remote(
            part(main_away, low_away, s, c), part(main_core, low_core, s, c),
            core_send.at[s, c], core_recv.at[s, c], twin, me,
        )

    def up_copy(s, c, to):
        return remote(
            part(main_send, low_send, s, c), part(main_lo, low_lo, s, c),
            line_send.at[s, c], lo_recv.at[s, c], to, me,
        )

    def down_copy(s, c, to):
        return remote(
            part(main_send, low_send, s, c), part(main_hi, low_hi, s, c),
            line_send.at[s, c], hi_recv.at[s, c], to, me,
        )

    def pair_sum(s, c):
        core_copy(s, c).wait_recv()
        return part(main_own, low_own, s, c)[...] + part(main_core, low_core, s, c)[...].astype(f32)

    messages = [(k, s) for k in range(chips - 2) for s in range(last)]
    early = len(messages)
    messages += [(k, last) for k in range(chips - 2)]
    messages += [(chips - 2, s) for s in range(last + 1)]

    def hop(z, up, k, s):
        c = chips - 1 - k if up else k
        total = pair_sum(s, c)
        if up and z > 0:
            up_copy(s, c, dp + 2).wait_recv()
            total = total + part(main_lo, low_lo, s, c)[...].astype(f32)
        if not up and z < chips - 1:
            down_copy(s, c, dp - 2).wait_recv()
            total = total + part(main_hi, low_hi, s, c)[...].astype(f32)
        part(main_send, low_send, s, c)[...] = total.astype(bf16)
        if up:
            up_copy(s, c, dp + 2).start()
        else:
            down_copy(s, c, dp - 2).start()

    def hops(z):
        found = []
        for index, (k, s) in enumerate(messages):
            for up in (True, False):
                depth = z if up else chips - 1 - z
                if depth < chips - 1 and k < chips - 1 - depth:
                    found.append((2 * depth + index, depth, up, k, s))
        return [event[2:] for event in sorted(found)]

    for level in range(last):
        main_terms(other_core, main_away, level)
        for c in far_first:
            core_copy(level, c).start()
    for level in range(last):
        main_terms(core, main_own, level)
    back_copies = []
    for bit in range(levels):
        back_own[bit] = dot_nn(hidden[...], w[bit + 1]).astype(bf16)
        copy = remote(
            back_own.at[bit], back_got.at[bit], back_send.at[bit], back_recv.at[bit],
            dp, mate(1 << bit),
        )
        copy.start()
        back_copies.append(copy)

    for z in sorted({0, chips - 1}):

        @pl.when(chip == z)
        def _():
            for event in hops(z)[:early]:
                hop(z, *event)

    for copy in lg_copies:
        copy.wait_recv()
    for k in range(n_width - 1):
        lg_mine = lg_mine + lg_got[k].astype(f32)
    latent_grad = lg_mine.astype(bf16)

    def low_terms(which, out_ref):
        lhs = x_t[:, which].reshape(chips * x_t.shape[2], rows)
        term = dot_nn(lhs, latent_grad).astype(out_ref.dtype)
        out_ref[...] = term.reshape(out_ref.shape)

    low_terms(other_core, low_away)
    for c in far_first:
        core_copy(last, c).start()
    low_terms(core, low_own)
    own_back[...] = dot_nn(hidden[...], w[0]) + dot_nt(latent_grad, left[...])
    for z in range(chips):

        @pl.when(chip == z)
        def _():
            events = hops(z)
            for event in events[early:] if z in (0, chips - 1) else events:
                hop(z, *event)

    total = own_back[...]
    for bit in range(levels):
        back_copies[bit].wait_recv()
        total = total + back_got[bit].astype(f32)
    in_out[...] = total.astype(bf16)

    for z in range(chips):

        @pl.when(chip == z)
        def _():
            for s in range(last + 1):
                total = pair_sum(s, z)
                if z > 0:
                    up_copy(s, z, dp - 2).wait_recv()
                    total = total + part(main_lo, low_lo, s, z)[...].astype(f32)
                if z < chips - 1:
                    down_copy(s, z, dp + 2).wait_recv()
                    total = total + part(main_hi, low_hi, s, z)[...].astype(f32)
                if s == last:
                    left_out[...] = total * scale
                else:
                    block_out[s] = total[:ob] * scale
                if s == levels:
                    right_out[...] = total[ob:] * scale

    for copy in x_copies + lat_copies + lg_copies + back_copies:
        copy.wait_send()
    for s in range(last + 1):
        for c in range(chips):
            core_copy(s, c).wait_send()

            @pl.when(chip != c)
            def _():
                up_copy(s, c, twin).wait_send()


def shards(inputs, block_weights, low_left, low_right, out_grad):
    n_dp, n_width = lax.axis_size("dp"), lax.axis_size("width")
    levels = n_width.bit_length() - 1
    rows, _, width_in = inputs.shape
    width_out = block_weights.shape[1]
    rank = low_left.shape[2]
    ob, ib, rb = width_out // n_dp, width_in // n_dp, rank // n_dp
    fits = n_dp % 2 == 0 and rows % 16 == 0 and width_in == width_out
    if not fits or ob % 16 or ib % 16 or rb % 16 or width_in % 128 or rank % 128:
        return plain_shards(inputs, block_weights, low_left, low_right, out_grad)
    chips = n_dp // 2
    scale = 1.0 / math.sqrt(rows * n_dp)
    main = (levels + 1) * ob + rb
    vm, dma = pltpu.VMEM, pltpu.SemaphoreType.DMA

    def line_scratch(r, c):
        return [
            vm((chips, r, c), bf16),
            vm((chips, r, c), f32),
            vm((chips, r, c), bf16),
            vm((chips, r, c), bf16),
            vm((chips, r, c), bf16),
            vm((chips, r, c), bf16),
        ]

    outs = pl.pallas_call(
        functools.partial(step_kernel, n_dp, n_width, scale),
        out_shape=(
            jax.ShapeDtypeStruct((rows, width_out), bf16),
            jax.ShapeDtypeStruct((rows, width_in), bf16),
            jax.ShapeDtypeStruct((levels + 1, ob, width_in), f32),
            jax.ShapeDtypeStruct((ib, rank), f32),
            jax.ShapeDtypeStruct((rb, width_out), f32),
        ),
        in_specs=[pl.BlockSpec(memory_space=pltpu.HBM)] * 5,
        out_specs=(pl.BlockSpec(memory_space=pltpu.VMEM),) * 5,
        scratch_shapes=[
            vm((rows, width_in), bf16),
            vm((levels + 1, width_out, width_in), bf16),
            vm((width_in, rank), bf16),
            vm((rank, width_out), bf16),
            vm((rows, width_out), bf16),
            vm((levels, rows, width_in), bf16),
            vm((rows, rank), bf16),
            vm((n_width - 1, rows, rank), bf16),
            vm((rows, rank), bf16),
            vm((n_width - 1, rows, rank), bf16),
            vm((rows, width_out), bf16),
            vm((chips, 2, ib, rows), bf16),
            vm((chips, 2, ob, rows), bf16),
            vm((chips, 2, rb, rows), bf16),
            vm((levels, rows, width_in), bf16),
            vm((levels, rows, width_in), bf16),
            vm((rows, width_out), f32),
            vm((rows, width_in), f32),
            *line_scratch(main, width_in),
            *line_scratch(ib, rank),
            dma((5,)),
            dma((levels,)),
            dma((levels,)),
            dma((n_width - 1,)),
            dma((n_width - 1,)),
            dma((n_width - 1,)),
            dma((n_width - 1,)),
            dma((levels,)),
            dma((levels,)),
            dma((levels + 2, chips)),
            dma((levels + 2, chips)),
            dma((levels + 2, chips)),
            dma((levels + 2, chips)),
            dma((levels + 2, chips)),
        ],
        compiler_params=pltpu.CompilerParams(
            collective_id=0, has_side_effects=True
        ),
    )(
        inputs[:, 0],
        block_weights[0].transpose(1, 0, 2),
        low_left[0],
        low_right[0],
        out_grad[:, 0],
    )
    act, in_grad, block, left, right = outs
    return (
        act[:, None],
        in_grad[:, None],
        block.transpose(1, 0, 2)[None],
        left[None],
        right[None],
    )


def solution(mesh):
    placed = (
        P("dp", "width", None),
        P("width", None, None, None),
        P("width", None, None),
        P("width", None, None),
        P("dp", "width", None),
    )
    return jax.shard_map(
        shards,
        mesh=mesh,
        in_specs=placed,
        out_specs=(
            P("dp", "width", None),
            P("dp", "width", None),
            P("width", "dp", None, None),
            P("width", "dp", None),
            P("width", "dp", None),
        ),
        check_vma=False,
    )
```

```python
import functools
import math

import jax
import jax.numpy as jnp
from jax import lax
from jax.experimental import pallas as pl
from jax.experimental.pallas import tpu as pltpu
from jax.sharding import PartitionSpec as P

root_half = 0.7071067811865476
inv_root_two_pi = 0.3989422804014327


def swapped(array, axis, apart):
    return lax.ppermute(array, axis, [(i, i ^ 1 << apart) for i in range(lax.axis_size(axis))])


def gelu_value(pre):
    return 0.5 * pre * (1.0 + lax.erf(pre * root_half))


def gelu_slope(pre):
    return (
        0.5 * (1.0 + lax.erf(pre * root_half)) + pre * jnp.exp(-0.5 * pre * pre) * inv_root_two_pi
    )


def plain_shards(inputs, block_weights, low_left, low_right, out_grad):
    own_x = inputs[:, 0]
    weights = block_weights[0]
    left = low_left[0]
    right = low_right[0]
    grad_out = out_grad[:, 0]
    levels = lax.axis_size("width").bit_length() - 1
    block_size = own_x.shape[1]
    scale = 1.0 / math.sqrt(own_x.shape[0] * lax.axis_size("dp"))
    pieces = [own_x]
    for bit in range(levels):
        pieces.append(swapped(own_x, "width", bit))
    all_x = jnp.stack(pieces, axis=1)
    latent = lax.psum(jnp.dot(own_x, left, preferred_element_type=jnp.float32), "width").astype(
        jnp.bfloat16
    )
    pre = lax.dot_general(
        all_x, weights, (((1, 2), (1, 2)), ((), ())), preferred_element_type=jnp.float32
    )
    pre = pre + jnp.dot(latent, right, preferred_element_type=jnp.float32)
    activations = gelu_value(pre).astype(jnp.bfloat16)
    hidden = (grad_out.astype(jnp.float32) * gelu_slope(pre)).astype(jnp.bfloat16)
    latent_term = lax.dot_general(
        hidden, right, (((1,), (1,)), ((), ())), preferred_element_type=jnp.float32
    )
    latent_grad = lax.psum(latent_term, "width").astype(jnp.bfloat16)
    partner_w = weights[:, 1:, :].reshape(weights.shape[0], levels * block_size)
    backs = jnp.dot(hidden, partner_w, preferred_element_type=jnp.float32).astype(jnp.bfloat16)
    returned = jnp.zeros(own_x.shape, jnp.float32)
    for bit in range(levels):
        piece = backs[:, bit * block_size : (bit + 1) * block_size]
        returned = returned + swapped(piece, "width", bit).astype(jnp.float32)
    own_back = jnp.dot(hidden, weights[:, 0, :], preferred_element_type=jnp.float32)
    own_back = own_back + lax.dot_general(
        latent_grad, left, (((1,), (1,)), ((), ())), preferred_element_type=jnp.float32
    )
    in_grad = (own_back + returned).astype(jnp.bfloat16)
    left_term = (
        lax.dot_general(
            own_x, latent_grad, (((0,), (0,)), ((), ())), preferred_element_type=jnp.float32
        )
        * scale
    )
    right_term = (
        lax.dot_general(
            latent, hidden, (((0,), (0,)), ((), ())), preferred_element_type=jnp.float32
        )
        * scale
    )
    block_term = (
        lax.dot_general(hidden, all_x, (((0,), (0,)), ((), ())), preferred_element_type=jnp.float32)
        * scale
    )
    block_grad, left_grad, right_grad = (
        lax.psum_scatter(block_term, "dp", scatter_dimension=0, tiled=True),
        lax.psum_scatter(left_term, "dp", scatter_dimension=0, tiled=True),
        lax.psum_scatter(right_term, "dp", scatter_dimension=0, tiled=True),
    )
    return (
        activations[:, None],
        in_grad[:, None],
        block_grad[None],
        left_grad[None],
        right_grad[None],
    )


f32 = jnp.float32
bf16 = jnp.bfloat16


def dot_nn(a, b):
    return jnp.dot(a, b, preferred_element_type=f32)


def dot_nt(a, b):
    return lax.dot_general(a, b, (((1,), (1,)), ((), ())), preferred_element_type=f32)


def remote(src, dst, send, recv, dp, width):
    return pltpu.make_async_remote_copy(
        src_ref=src,
        dst_ref=dst,
        send_sem=send,
        recv_sem=recv,
        device_id={"dp": dp, "width": width},
        device_id_type=pl.DeviceIdType.MESH,
    )


def step_kernel(
    n_dp, n_width, scale,
    x_hbm, w_hbm, left_hbm, right_hbm, g_hbm,
    act_out, in_out, block_out, left_out, right_out,
    x, w, left, right, g,
    xs, lat_own, lat_got, lg_own, lg_got, hidden, x_t, h_t, lat_t,
    back_own, back_got, pre, own_back,
    main_away, main_own, main_core, main_send, main_lo, main_hi,
    low_away, low_own, low_core, low_send, low_lo, low_hi,
    load_sem, x_send, x_recv, lat_send, lat_recv, lg_send, lg_recv, back_send, back_recv,
    core_send, core_recv, line_send, lo_recv, hi_recv,
):
    levels = n_width.bit_length() - 1
    chips = n_dp // 2
    dp = lax.axis_index("dp")
    me = lax.axis_index("width")
    chip, core = dp // 2, dp % 2
    other_core = 1 - core
    twin = dp + 1 - 2 * core

    def mate(k):
        at = me
        for bit in range(levels):
            if k >> bit & 1:
                at = at + (1 << bit) * (1 - 2 * ((me // (1 << bit)) % 2))
        return at

    barrier = pltpu.get_barrier_semaphore()

    def greet(to_dp, to_width):
        pl.semaphore_signal(
            barrier,
            inc=1,
            device_id={"dp": to_dp, "width": to_width},
            device_id_type=pl.DeviceIdType.MESH,
        )

    for k in range(1, n_width):
        greet(dp, mate(k))
    greet(twin, me)

    @pl.when(chip > 0)
    def _():
        greet(dp - 2, me)

    @pl.when(chip < chips - 1)
    def _():
        greet(dp + 2, me)

    loads = [
        pltpu.make_async_copy(src, dst, load_sem.at[i])
        for i, (src, dst) in enumerate(
            ((x_hbm, x), (left_hbm, left), (w_hbm, w), (right_hbm, right), (g_hbm, g))
        )
    ]
    for load in loads:
        load.start()

    ends = jnp.where(chip == 0, 1, 0) + jnp.where(chip == chips - 1, 1, 0)
    pl.semaphore_wait(barrier, n_width + 2 - ends)

    loads[0].wait()
    x_copies = [
        remote(x, xs.at[bit], x_send.at[bit], x_recv.at[bit], dp, mate(1 << bit))
        for bit in range(levels)
    ]
    loads[1].wait()
    lat_mine = dot_nn(x[...], left[...])
    lat_own[...] = lat_mine.astype(bf16)
    lat_copies = [
        remote(lat_own, lat_got.at[k - 1], lat_send.at[k - 1], lat_recv.at[k - 1], dp, mate(k))
        for k in range(1, n_width)
    ]
    for copy in lat_copies:
        copy.start()
    for copy in x_copies:
        copy.start()
    loads[2].wait()
    pre[...] = dot_nt(x[...], w[0])
    x_t[...] = x[...].astype(f32).T.astype(bf16).reshape(x_t.shape)
    loads[3].wait()
    loads[4].wait()
    for copy in lat_copies:
        copy.wait_recv()
    lat_sum = lat_mine
    for k in range(n_width - 1):
        lat_sum = lat_sum + lat_got[k].astype(f32)
    latent = lat_sum.astype(bf16)
    lat_t[...] = lat_sum.T.astype(bf16).reshape(lat_t.shape)
    pre[...] += dot_nn(latent, right[...])
    for bit in range(levels):
        x_copies[bit].wait_recv()
        pre[...] += dot_nt(xs[bit], w[bit + 1])

    v = pre[...]
    half = 0.5 * (1.0 + lax.erf(v * root_half))
    act_out[...] = (v * half).astype(bf16)
    slope = half + v * jnp.exp(-0.5 * v * v) * inv_root_two_pi
    hid = g[...].astype(f32) * slope
    hidden[...] = hid.astype(bf16)
    h = hidden[...]
    lg_mine = dot_nt(h, right[...])
    lg_own[...] = lg_mine.astype(bf16)
    lg_copies = [
        remote(lg_own, lg_got.at[k - 1], lg_send.at[k - 1], lg_recv.at[k - 1], dp, mate(k))
        for k in range(1, n_width)
    ]
    for copy in lg_copies:
        copy.start()
    h_t[...] = h.astype(f32).T.astype(bf16).reshape(h_t.shape)

    ob, rb = h_t.shape[2], lat_t.shape[2]
    rows = h_t.shape[3]

    last = levels + 1

    def main_terms(which, out_ref, level):
        lhs = h_t[:, which].reshape(chips * ob, rows)
        rhs = x[...] if level == 0 else xs[level - 1]
        term = dot_nn(lhs, rhs).astype(out_ref.dtype)
        out_ref[:, level * ob : (level + 1) * ob, :] = term.reshape(chips, ob, term.shape[1])
        if level == levels:
            lhs = lat_t[:, which].reshape(chips * rb, rows)
            term = dot_nn(lhs, hidden[...]).astype(out_ref.dtype)
            out_ref[:, last * ob :, :] = term.reshape(chips, rb, term.shape[1])

    far_first = []
    for k in range((chips + 1) // 2):
        far_first += [chips - 1 - k, k] if chips - 1 - k != k else [k]

    def part(main_ref, low_ref, s, c):
        if s == last:
            return low_ref.at[c]
        top = (s + 1) * ob + (rb if s == levels else 0)
        return main_ref.at[c, s * ob : top]

    def core_copy(s, c):
        return remote(
            part(main_away, low_away, s, c), part(main_core, low_core, s, c),
            core_send.at[s, c], core_recv.at[s, c], twin, me,
        )

    def up_copy(s, c, to):
        return remote(
            part(main_send, low_send, s, c), part(main_lo, low_lo, s, c),
            line_send.at[s, c], lo_recv.at[s, c], to, me,
        )

    def down_copy(s, c, to):
        return remote(
            part(main_send, low_send, s, c), part(main_hi, low_hi, s, c),
            line_send.at[s, c], hi_recv.at[s, c], to, me,
        )

    def pair_sum(s, c):
        core_copy(s, c).wait_recv()
        return part(main_own, low_own, s, c)[...] + part(main_core, low_core, s, c)[...].astype(f32)

    messages = [(k, s) for k in range(chips - 2) for s in range(last)]
    early = len(messages)
    messages += [(k, last) for k in range(chips - 2)]
    messages += [(chips - 2, s) for s in range(last + 1)]

    def hop(z, up, k, s):
        c = chips - 1 - k if up else k
        total = pair_sum(s, c)
        if up and z > 0:
            up_copy(s, c, dp + 2).wait_recv()
            total = total + part(main_lo, low_lo, s, c)[...].astype(f32)
        if not up and z < chips - 1:
            down_copy(s, c, dp - 2).wait_recv()
            total = total + part(main_hi, low_hi, s, c)[...].astype(f32)
        part(main_send, low_send, s, c)[...] = total.astype(bf16)
        if up:
            up_copy(s, c, dp + 2).start()
        else:
            down_copy(s, c, dp - 2).start()

    def hops(z):
        found = []
        for index, (k, s) in enumerate(messages):
            for up in (True, False):
                depth = z if up else chips - 1 - z
                if depth < chips - 1 and k < chips - 1 - depth:
                    found.append((2 * depth + index, depth, up, k, s))
        return [event[2:] for event in sorted(found)]

    for level in range(last):
        main_terms(other_core, main_away, level)
        for c in far_first:
            core_copy(level, c).start()
    for level in range(last):
        main_terms(core, main_own, level)
    back_copies = []
    for bit in range(levels):
        back_own[bit] = dot_nn(hidden[...], w[bit + 1]).astype(bf16)
        copy = remote(
            back_own.at[bit], back_got.at[bit], back_send.at[bit], back_recv.at[bit],
            dp, mate(1 << bit),
        )
        copy.start()
        back_copies.append(copy)

    for z in sorted({0, chips - 1}):

        @pl.when(chip == z)
        def _():
            for event in hops(z)[:early]:
                hop(z, *event)

    for copy in lg_copies:
        copy.wait_recv()
    for k in range(n_width - 1):
        lg_mine = lg_mine + lg_got[k].astype(f32)
    latent_grad = lg_mine.astype(bf16)

    def low_terms(which, out_ref):
        lhs = x_t[:, which].reshape(chips * x_t.shape[2], rows)
        term = dot_nn(lhs, latent_grad).astype(out_ref.dtype)
        out_ref[...] = term.reshape(out_ref.shape)

    low_terms(other_core, low_away)
    for c in far_first:
        core_copy(last, c).start()
    low_terms(core, low_own)
    own_back[...] = dot_nn(hidden[...], w[0]) + dot_nt(latent_grad, left[...])
    for z in range(chips):

        @pl.when(chip == z)
        def _():
            events = hops(z)
            for event in events[early:] if z in (0, chips - 1) else events:
                hop(z, *event)

    total = own_back[...]
    for bit in range(levels):
        back_copies[bit].wait_recv()
        total = total + back_got[bit].astype(f32)
    in_out[...] = total.astype(bf16)

    for z in range(chips):

        @pl.when(chip == z)
        def _():
            for s in range(last + 1):
                total = pair_sum(s, z)
                if z > 0:
                    up_copy(s, z, dp - 2).wait_recv()
                    total = total + part(main_lo, low_lo, s, z)[...].astype(f32)
                if z < chips - 1:
                    down_copy(s, z, dp + 2).wait_recv()
                    total = total + part(main_hi, low_hi, s, z)[...].astype(f32)
                if s == last:
                    left_out[...] = total * scale
                else:
                    block_out[s] = total[:ob] * scale
                if s == levels:
                    right_out[...] = total[ob:] * scale

    for copy in x_copies + lat_copies + lg_copies + back_copies:
        copy.wait_send()
    for s in range(last + 1):
        for c in range(chips):
            core_copy(s, c).wait_send()

            @pl.when(chip != c)
            def _():
                up_copy(s, c, twin).wait_send()


def hand_over(*refs):
    copies = [pltpu.make_async_copy(refs[i], refs[5 + i], refs[10].at[i]) for i in range(5)]
    for copy in copies:
        copy.start()
    for copy in copies:
        copy.wait()


def shards(inputs, block_weights, low_left, low_right, out_grad):
    n_dp, n_width = lax.axis_size("dp"), lax.axis_size("width")
    levels = n_width.bit_length() - 1
    rows, _, width_in = inputs.shape
    width_out = block_weights.shape[1]
    rank = low_left.shape[2]
    ob, ib, rb = width_out // n_dp, width_in // n_dp, rank // n_dp
    fits = n_dp % 2 == 0 and rows % 16 == 0 and width_in == width_out
    if not fits or ob % 16 or ib % 16 or rb % 16 or width_in % 128 or rank % 128:
        return plain_shards(inputs, block_weights, low_left, low_right, out_grad)
    chips = n_dp // 2
    scale = 1.0 / math.sqrt(rows * n_dp)
    main = (levels + 1) * ob + rb
    vm, dma = pltpu.VMEM, pltpu.SemaphoreType.DMA

    def line_scratch(r, c):
        return [
            vm((chips, r, c), bf16),
            vm((chips, r, c), f32),
            vm((chips, r, c), bf16),
            vm((chips, r, c), bf16),
            vm((chips, r, c), bf16),
            vm((chips, r, c), bf16),
        ]

    outs = pl.pallas_call(
        functools.partial(step_kernel, n_dp, n_width, scale),
        out_shape=(
            jax.ShapeDtypeStruct((rows, width_out), bf16),
            jax.ShapeDtypeStruct((rows, width_in), bf16),
            jax.ShapeDtypeStruct((levels + 1, ob, width_in), f32),
            jax.ShapeDtypeStruct((ib, rank), f32),
            jax.ShapeDtypeStruct((rb, width_out), f32),
        ),
        in_specs=[pl.BlockSpec(memory_space=pltpu.HBM)] * 5,
        out_specs=(pl.BlockSpec(memory_space=pltpu.VMEM),) * 5,
        scratch_shapes=[
            vm((rows, width_in), bf16),
            vm((levels + 1, width_out, width_in), bf16),
            vm((width_in, rank), bf16),
            vm((rank, width_out), bf16),
            vm((rows, width_out), bf16),
            vm((levels, rows, width_in), bf16),
            vm((rows, rank), bf16),
            vm((n_width - 1, rows, rank), bf16),
            vm((rows, rank), bf16),
            vm((n_width - 1, rows, rank), bf16),
            vm((rows, width_out), bf16),
            vm((chips, 2, ib, rows), bf16),
            vm((chips, 2, ob, rows), bf16),
            vm((chips, 2, rb, rows), bf16),
            vm((levels, rows, width_in), bf16),
            vm((levels, rows, width_in), bf16),
            vm((rows, width_out), f32),
            vm((rows, width_in), f32),
            *line_scratch(main, width_in),
            *line_scratch(ib, rank),
            dma((5,)),
            dma((levels,)),
            dma((levels,)),
            dma((n_width - 1,)),
            dma((n_width - 1,)),
            dma((n_width - 1,)),
            dma((n_width - 1,)),
            dma((levels,)),
            dma((levels,)),
            dma((levels + 2, chips)),
            dma((levels + 2, chips)),
            dma((levels + 2, chips)),
            dma((levels + 2, chips)),
            dma((levels + 2, chips)),
        ],
        compiler_params=pltpu.CompilerParams(
            collective_id=0, has_side_effects=True, vmem_limit_bytes=40 * 1024 * 1024
        ),
    )(
        *(
            pltpu.with_memory_space_constraint(array, pltpu.HBM)
            for array in (
                inputs[:, 0],
                block_weights[0].transpose(1, 0, 2),
                low_left[0],
                low_right[0],
                out_grad[:, 0],
            )
        )
    )
    act, in_grad, block, left, right = pl.pallas_call(
        hand_over,
        out_shape=tuple(jax.ShapeDtypeStruct(out.shape, out.dtype) for out in outs),
        in_specs=[pl.BlockSpec(memory_space=pltpu.VMEM)] * 5,
        out_specs=(pl.BlockSpec(memory_space=pl.ANY),) * 5,
        scratch_shapes=[dma((5,))],
        compiler_params=pltpu.CompilerParams(vmem_limit_bytes=4 * 1024 * 1024),
    )(*outs)
    return (
        act[:, None],
        in_grad[:, None],
        block.transpose(1, 0, 2)[None],
        left[None],
        right[None],
    )


def solution(mesh):
    placed = (
        P("dp", "width", None),
        P("width", None, None, None),
        P("width", None, None),
        P("width", None, None),
        P("dp", "width", None),
    )
    return jax.shard_map(
        shards,
        mesh=mesh,
        in_specs=placed,
        out_specs=(
            P("dp", "width", None),
            P("dp", "width", None),
            P("width", "dp", None, None),
            P("width", "dp", None),
            P("width", "dp", None),
        ),
        check_vma=False,
    )
```

```python
import functools
import math

import jax
import jax.numpy as jnp
from jax import lax
from jax.experimental import pallas as pl
from jax.experimental.pallas import tpu as pltpu
from jax.sharding import PartitionSpec as P

root_half = 0.7071067811865476
inv_root_two_pi = 0.3989422804014327


def swapped(array, axis, apart):
    return lax.ppermute(array, axis, [(i, i ^ 1 << apart) for i in range(lax.axis_size(axis))])


def gelu_value(pre):
    return 0.5 * pre * (1.0 + lax.erf(pre * root_half))


def gelu_slope(pre):
    return (
        0.5 * (1.0 + lax.erf(pre * root_half)) + pre * jnp.exp(-0.5 * pre * pre) * inv_root_two_pi
    )


def plain_shards(inputs, block_weights, low_left, low_right, out_grad):
    own_x = inputs[:, 0]
    weights = block_weights[0]
    left = low_left[0]
    right = low_right[0]
    grad_out = out_grad[:, 0]
    levels = lax.axis_size("width").bit_length() - 1
    block_size = own_x.shape[1]
    scale = 1.0 / math.sqrt(own_x.shape[0] * lax.axis_size("dp"))
    pieces = [own_x]
    for bit in range(levels):
        pieces.append(swapped(own_x, "width", bit))
    all_x = jnp.stack(pieces, axis=1)
    latent = lax.psum(jnp.dot(own_x, left, preferred_element_type=jnp.float32), "width").astype(
        jnp.bfloat16
    )
    pre = lax.dot_general(
        all_x, weights, (((1, 2), (1, 2)), ((), ())), preferred_element_type=jnp.float32
    )
    pre = pre + jnp.dot(latent, right, preferred_element_type=jnp.float32)
    activations = gelu_value(pre).astype(jnp.bfloat16)
    hidden = (grad_out.astype(jnp.float32) * gelu_slope(pre)).astype(jnp.bfloat16)
    latent_term = lax.dot_general(
        hidden, right, (((1,), (1,)), ((), ())), preferred_element_type=jnp.float32
    )
    latent_grad = lax.psum(latent_term, "width").astype(jnp.bfloat16)
    partner_w = weights[:, 1:, :].reshape(weights.shape[0], levels * block_size)
    backs = jnp.dot(hidden, partner_w, preferred_element_type=jnp.float32).astype(jnp.bfloat16)
    returned = jnp.zeros(own_x.shape, jnp.float32)
    for bit in range(levels):
        piece = backs[:, bit * block_size : (bit + 1) * block_size]
        returned = returned + swapped(piece, "width", bit).astype(jnp.float32)
    own_back = jnp.dot(hidden, weights[:, 0, :], preferred_element_type=jnp.float32)
    own_back = own_back + lax.dot_general(
        latent_grad, left, (((1,), (1,)), ((), ())), preferred_element_type=jnp.float32
    )
    in_grad = (own_back + returned).astype(jnp.bfloat16)
    left_term = (
        lax.dot_general(
            own_x, latent_grad, (((0,), (0,)), ((), ())), preferred_element_type=jnp.float32
        )
        * scale
    )
    right_term = (
        lax.dot_general(
            latent, hidden, (((0,), (0,)), ((), ())), preferred_element_type=jnp.float32
        )
        * scale
    )
    block_term = (
        lax.dot_general(hidden, all_x, (((0,), (0,)), ((), ())), preferred_element_type=jnp.float32)
        * scale
    )
    block_grad, left_grad, right_grad = (
        lax.psum_scatter(block_term, "dp", scatter_dimension=0, tiled=True),
        lax.psum_scatter(left_term, "dp", scatter_dimension=0, tiled=True),
        lax.psum_scatter(right_term, "dp", scatter_dimension=0, tiled=True),
    )
    return (
        activations[:, None],
        in_grad[:, None],
        block_grad[None],
        left_grad[None],
        right_grad[None],
    )


f32 = jnp.float32
bf16 = jnp.bfloat16


def dot_nn(a, b):
    return jnp.dot(a, b, preferred_element_type=f32)


def dot_nt(a, b):
    return lax.dot_general(a, b, (((1,), (1,)), ((), ())), preferred_element_type=f32)


def remote(src, dst, send, recv, dp, width):
    return pltpu.make_async_remote_copy(
        src_ref=src,
        dst_ref=dst,
        send_sem=send,
        recv_sem=recv,
        device_id={"dp": dp, "width": width},
        device_id_type=pl.DeviceIdType.MESH,
    )


def step_kernel(
    n_dp, n_width, scale,
    x_hbm, w_hbm, left_hbm, right_hbm, g_hbm,
    act_out, in_out, block_out, left_out, right_out,
    x, w, left, right, g,
    xs, lat_sum, lat_own, lat_got, lat_full, lg_own, lg_got, hidden, x_t, h_t, lat_t,
    back_own, back_got, pre, own_back,
    main_away, main_own, main_core, main_send, main_lo, main_hi,
    low_away, low_own, low_core, low_send, low_lo, low_hi,
    load_sem, x_send, x_recv, lat_send, lat_recv, lg_send, lg_recv, back_send, back_recv,
    core_send, core_recv, line_send, lo_recv, hi_recv,
):
    levels = n_width.bit_length() - 1
    chips = n_dp // 2
    dp = lax.axis_index("dp")
    me = lax.axis_index("width")
    chip, core = dp // 2, dp % 2
    other_core = 1 - core
    twin = dp + 1 - 2 * core

    def mate(k):
        at = me
        for bit in range(levels):
            if k >> bit & 1:
                at = at + (1 << bit) * (1 - 2 * ((me // (1 << bit)) % 2))
        return at

    barrier = pltpu.get_barrier_semaphore()

    def greet(to_dp, to_width):
        pl.semaphore_signal(
            barrier,
            inc=1,
            device_id={"dp": to_dp, "width": to_width},
            device_id_type=pl.DeviceIdType.MESH,
        )

    for k in range(1, n_width):
        greet(dp, mate(k))
    greet(twin, me)

    @pl.when(chip > 0)
    def _():
        greet(dp - 2, me)

    @pl.when(chip < chips - 1)
    def _():
        greet(dp + 2, me)

    loads = [
        pltpu.make_async_copy(src, dst, load_sem.at[i])
        for i, (src, dst) in enumerate(
            ((x_hbm, x), (left_hbm, left), (w_hbm, w), (right_hbm, right), (g_hbm, g))
        )
    ]
    for load in loads:
        load.start()

    ends = jnp.where(chip == 0, 1, 0) + jnp.where(chip == chips - 1, 1, 0)
    pl.semaphore_wait(barrier, n_width + 2 - ends)

    loads[0].wait()
    tall = x.shape[0]
    share = tall // n_width
    halves = [slice(0, tall // 2), slice(tall // 2, tall)]
    x_copies = [
        [
            remote(
                x.at[half], xs.at[bit, half], x_send.at[part, bit], x_recv.at[part, bit],
                dp, mate(1 << bit),
            )
            for bit in range(levels)
        ]
        for part, half in enumerate(halves)
    ]

    def rows_of(device):
        return pl.ds(pl.multiple_of(device * share, share), share)

    loads[1].wait()
    lat_sum[...] = dot_nn(x[...], left[...])
    lat_own[...] = lat_sum[...].astype(bf16)
    lat_copies = [
        remote(
            lat_own.at[rows_of(mate(k))], lat_got.at[k - 1],
            lat_send.at[0, k - 1], lat_recv.at[0, k - 1], dp, mate(k),
        )
        for k in range(1, n_width)
    ]
    for copy in lat_copies + x_copies[0]:
        copy.start()
    loads[2].wait()
    pre[...] = dot_nt(x[...], w[0])
    for copy in lat_copies:
        copy.wait_recv()
    mine = lat_sum[rows_of(me), :]
    for k in range(n_width - 1):
        mine = mine + lat_got[k].astype(f32)
    lat_full[rows_of(me), :] = mine.astype(bf16)
    full_copies = [
        remote(
            lat_full.at[rows_of(me)], lat_full.at[rows_of(me)],
            lat_send.at[1, k - 1], lat_recv.at[1, k - 1], dp, mate(k),
        )
        for k in range(1, n_width)
    ]
    for copy in full_copies + x_copies[1]:
        copy.start()
    x_t[...] = x[...].astype(f32).T.astype(bf16).reshape(x_t.shape)
    loads[3].wait()
    loads[4].wait()
    for k in range(1, n_width):
        remote(
            lat_full.at[rows_of(mate(k))], lat_full.at[rows_of(mate(k))],
            lat_send.at[1, k - 1], lat_recv.at[1, k - 1], dp, mate(k),
        ).wait_recv()
    latent = lat_full[...]
    lat_t[...] = latent.astype(f32).T.astype(bf16).reshape(lat_t.shape)
    pre[...] += dot_nn(latent, right[...])
    for bit in range(levels):
        for part in range(2):
            x_copies[part][bit].wait_recv()
        pre[...] += dot_nt(xs[bit], w[bit + 1])

    v = pre[...]
    half = 0.5 * (1.0 + lax.erf(v * root_half))
    act_out[...] = (v * half).astype(bf16)
    slope = half + v * jnp.exp(-0.5 * v * v) * inv_root_two_pi
    hid = g[...].astype(f32) * slope
    hidden[...] = hid.astype(bf16)
    h = hidden[...]
    lg_mine = dot_nt(h, right[...])
    lg_own[...] = lg_mine.astype(bf16)
    lg_copies = [
        remote(lg_own, lg_got.at[k - 1], lg_send.at[k - 1], lg_recv.at[k - 1], dp, mate(k))
        for k in range(1, n_width)
    ]
    for copy in lg_copies:
        copy.start()
    h_t[...] = h.astype(f32).T.astype(bf16).reshape(h_t.shape)

    ob, rb = h_t.shape[2], lat_t.shape[2]
    rows = h_t.shape[3]

    last = levels + 1

    def main_terms(which, out_ref, level):
        lhs = h_t[:, which].reshape(chips * ob, rows)
        rhs = x[...] if level == 0 else xs[level - 1]
        term = dot_nn(lhs, rhs).astype(out_ref.dtype)
        out_ref[:, level * ob : (level + 1) * ob, :] = term.reshape(chips, ob, term.shape[1])
        if level == levels:
            lhs = lat_t[:, which].reshape(chips * rb, rows)
            term = dot_nn(lhs, hidden[...]).astype(out_ref.dtype)
            out_ref[:, last * ob :, :] = term.reshape(chips, rb, term.shape[1])

    far_first = []
    for k in range((chips + 1) // 2):
        far_first += [chips - 1 - k, k] if chips - 1 - k != k else [k]

    def part(main_ref, low_ref, s, c):
        if s == last:
            return low_ref.at[c]
        top = (s + 1) * ob + (rb if s == levels else 0)
        return main_ref.at[c, s * ob : top]

    def core_copy(s, c):
        return remote(
            part(main_away, low_away, s, c), part(main_core, low_core, s, c),
            core_send.at[s, c], core_recv.at[s, c], twin, me,
        )

    def up_copy(s, c, to):
        return remote(
            part(main_send, low_send, s, c), part(main_lo, low_lo, s, c),
            line_send.at[s, c], lo_recv.at[s, c], to, me,
        )

    def down_copy(s, c, to):
        return remote(
            part(main_send, low_send, s, c), part(main_hi, low_hi, s, c),
            line_send.at[s, c], hi_recv.at[s, c], to, me,
        )

    def pair_sum(s, c):
        core_copy(s, c).wait_recv()
        return part(main_own, low_own, s, c)[...] + part(main_core, low_core, s, c)[...].astype(f32)

    messages = [(k, s) for k in range(chips - 2) for s in range(last)]
    early = len(messages)
    messages += [(k, last) for k in range(chips - 2)]
    messages += [(chips - 2, s) for s in range(last + 1)]

    def hop(z, up, k, s):
        c = chips - 1 - k if up else k
        total = pair_sum(s, c)
        if up and z > 0:
            up_copy(s, c, dp + 2).wait_recv()
            total = total + part(main_lo, low_lo, s, c)[...].astype(f32)
        if not up and z < chips - 1:
            down_copy(s, c, dp - 2).wait_recv()
            total = total + part(main_hi, low_hi, s, c)[...].astype(f32)
        part(main_send, low_send, s, c)[...] = total.astype(bf16)
        if up:
            up_copy(s, c, dp + 2).start()
        else:
            down_copy(s, c, dp - 2).start()

    def hops(z):
        found = []
        for index, (k, s) in enumerate(messages):
            for up in (True, False):
                depth = z if up else chips - 1 - z
                if depth < chips - 1 and k < chips - 1 - depth:
                    found.append((2 * depth + index, depth, up, k, s))
        return [event[2:] for event in sorted(found)]

    for level in range(last):
        main_terms(other_core, main_away, level)
        for c in far_first:
            core_copy(level, c).start()
    for level in range(last):
        main_terms(core, main_own, level)
    back_copies = []
    for bit in range(levels):
        back_own[bit] = dot_nn(hidden[...], w[bit + 1]).astype(bf16)
        copy = remote(
            back_own.at[bit], back_got.at[bit], back_send.at[bit], back_recv.at[bit],
            dp, mate(1 << bit),
        )
        copy.start()
        back_copies.append(copy)

    for z in sorted({0, chips - 1}):

        @pl.when(chip == z)
        def _():
            for event in hops(z)[:early]:
                hop(z, *event)

    for copy in lg_copies:
        copy.wait_recv()
    for k in range(n_width - 1):
        lg_mine = lg_mine + lg_got[k].astype(f32)
    latent_grad = lg_mine.astype(bf16)

    def low_terms(which, out_ref):
        lhs = x_t[:, which].reshape(chips * x_t.shape[2], rows)
        term = dot_nn(lhs, latent_grad).astype(out_ref.dtype)
        out_ref[...] = term.reshape(out_ref.shape)

    low_terms(other_core, low_away)
    for c in far_first:
        core_copy(last, c).start()
    low_terms(core, low_own)
    own_back[...] = dot_nn(hidden[...], w[0]) + dot_nt(latent_grad, left[...])
    for z in range(chips):

        @pl.when(chip == z)
        def _():
            events = hops(z)
            for event in events[early:] if z in (0, chips - 1) else events:
                hop(z, *event)

    total = own_back[...]
    for bit in range(levels):
        back_copies[bit].wait_recv()
        total = total + back_got[bit].astype(f32)
    in_out[...] = total.astype(bf16)

    for z in range(chips):

        @pl.when(chip == z)
        def _():
            for s in range(last + 1):
                total = pair_sum(s, z)
                if z > 0:
                    up_copy(s, z, dp - 2).wait_recv()
                    total = total + part(main_lo, low_lo, s, z)[...].astype(f32)
                if z < chips - 1:
                    down_copy(s, z, dp + 2).wait_recv()
                    total = total + part(main_hi, low_hi, s, z)[...].astype(f32)
                if s == last:
                    left_out[...] = total * scale
                else:
                    block_out[s] = total[:ob] * scale
                if s == levels:
                    right_out[...] = total[ob:] * scale

    for copy in x_copies[0] + x_copies[1] + lat_copies + full_copies + lg_copies + back_copies:
        copy.wait_send()
    for s in range(last + 1):
        for c in range(chips):
            core_copy(s, c).wait_send()

            @pl.when(chip != c)
            def _():
                up_copy(s, c, twin).wait_send()


def hand_over(*refs):
    copies = [pltpu.make_async_copy(refs[i], refs[5 + i], refs[10].at[i]) for i in range(5)]
    for copy in copies:
        copy.start()
    for copy in copies:
        copy.wait()


def shards(inputs, block_weights, low_left, low_right, out_grad):
    n_dp, n_width = lax.axis_size("dp"), lax.axis_size("width")
    levels = n_width.bit_length() - 1
    rows, _, width_in = inputs.shape
    width_out = block_weights.shape[1]
    rank = low_left.shape[2]
    ob, ib, rb = width_out // n_dp, width_in // n_dp, rank // n_dp
    fits = n_dp % 2 == 0 and rows % (16 * n_width) == 0 and rows % 32 == 0 and width_in == width_out
    if not fits or ob % 16 or ib % 16 or rb % 16 or width_in % 128 or rank % 128:
        return plain_shards(inputs, block_weights, low_left, low_right, out_grad)
    chips = n_dp // 2
    scale = 1.0 / math.sqrt(rows * n_dp)
    main = (levels + 1) * ob + rb
    vm, dma = pltpu.VMEM, pltpu.SemaphoreType.DMA

    def line_scratch(r, c):
        return [
            vm((chips, r, c), bf16),
            vm((chips, r, c), f32),
            vm((chips, r, c), bf16),
            vm((chips, r, c), bf16),
            vm((chips, r, c), bf16),
            vm((chips, r, c), bf16),
        ]

    outs = pl.pallas_call(
        functools.partial(step_kernel, n_dp, n_width, scale),
        out_shape=(
            jax.ShapeDtypeStruct((rows, width_out), bf16),
            jax.ShapeDtypeStruct((rows, width_in), bf16),
            jax.ShapeDtypeStruct((levels + 1, ob, width_in), f32),
            jax.ShapeDtypeStruct((ib, rank), f32),
            jax.ShapeDtypeStruct((rb, width_out), f32),
        ),
        in_specs=[pl.BlockSpec(memory_space=pltpu.HBM)] * 5,
        out_specs=(pl.BlockSpec(memory_space=pltpu.VMEM),) * 5,
        scratch_shapes=[
            vm((rows, width_in), bf16),
            vm((levels + 1, width_out, width_in), bf16),
            vm((width_in, rank), bf16),
            vm((rank, width_out), bf16),
            vm((rows, width_out), bf16),
            vm((levels, rows, width_in), bf16),
            vm((rows, rank), f32),
            vm((rows, rank), bf16),
            vm((n_width - 1, rows // n_width, rank), bf16),
            vm((rows, rank), bf16),
            vm((rows, rank), bf16),
            vm((n_width - 1, rows, rank), bf16),
            vm((rows, width_out), bf16),
            vm((chips, 2, ib, rows), bf16),
            vm((chips, 2, ob, rows), bf16),
            vm((chips, 2, rb, rows), bf16),
            vm((levels, rows, width_in), bf16),
            vm((levels, rows, width_in), bf16),
            vm((rows, width_out), f32),
            vm((rows, width_in), f32),
            *line_scratch(main, width_in),
            *line_scratch(ib, rank),
            dma((5,)),
            dma((2, levels)),
            dma((2, levels)),
            dma((2, n_width - 1)),
            dma((2, n_width - 1)),
            dma((n_width - 1,)),
            dma((n_width - 1,)),
            dma((levels,)),
            dma((levels,)),
            dma((levels + 2, chips)),
            dma((levels + 2, chips)),
            dma((levels + 2, chips)),
            dma((levels + 2, chips)),
            dma((levels + 2, chips)),
        ],
        compiler_params=pltpu.CompilerParams(
            collective_id=0, has_side_effects=True, vmem_limit_bytes=40 * 1024 * 1024
        ),
    )(
        *(
            pltpu.with_memory_space_constraint(array, pltpu.HBM)
            for array in (
                inputs[:, 0],
                block_weights[0].transpose(1, 0, 2),
                low_left[0],
                low_right[0],
                out_grad[:, 0],
            )
        )
    )
    act, in_grad, block, left, right = pl.pallas_call(
        hand_over,
        out_shape=tuple(jax.ShapeDtypeStruct(out.shape, out.dtype) for out in outs),
        in_specs=[pl.BlockSpec(memory_space=pltpu.VMEM)] * 5,
        out_specs=(pl.BlockSpec(memory_space=pl.ANY),) * 5,
        scratch_shapes=[dma((5,))],
        compiler_params=pltpu.CompilerParams(vmem_limit_bytes=4 * 1024 * 1024),
    )(*outs)
    return (
        act[:, None],
        in_grad[:, None],
        block.transpose(1, 0, 2)[None],
        left[None],
        right[None],
    )


def solution(mesh):
    placed = (
        P("dp", "width", None),
        P("width", None, None, None),
        P("width", None, None),
        P("width", None, None),
        P("dp", "width", None),
    )
    return jax.shard_map(
        shards,
        mesh=mesh,
        in_specs=placed,
        out_specs=(
            P("dp", "width", None),
            P("dp", "width", None),
            P("width", "dp", None, None),
            P("width", "dp", None),
            P("width", "dp", None),
        ),
        check_vma=False,
    )
```
